32 devices in a mesh: day: 2 (over x), chan: 16 (over z, y, core).
Axes of the slice: x: 2, y: 2, z: 4, core: 2. Of those that a mesh axis runs over, the one named last changes fastest.
Arguments:
- records: bfloat16 [1024, 8, 3000], P(('day', 'chan')), parts along dimension 0, may hold values from -6 to 6
- live_mask: int32 [1024], P(('day', 'chan')), parts along dimension 0, may hold values 0 or 1
- offsets: int32 [16], replicated, may hold values from 1 to 511, as said below
Outputs:
- correlations: bfloat16 [1024, 16, 2048], P(('day', 'chan')), parts along dimension 0
The draws below stay inside these ranges and needn't reach their ends.
There are 2 independent parts, one for each index of `day`. The reference program is written for one: setup_inputs(seed, part) draws one part's arguments, and reference() takes and returns one part's arrays. A program takes and returns all parts, laid end to end along the dimension named above; an argument that names none is the same for every part. Nothing has to cross between parts.
Inputs may be any that keep to these rules, and one draw needn't show every extreme that they name: offsets[k] lies between k * 32 + 1 and (k + 1) * 32, and the last one equals 511.
All inputs are finite; a program needn't handle non-finite values. No bound on the sum of `live_mask` on one device may be relied on, other than what follows from the above.
Results may differ from the reference program's by a relative error of at most 0.0076.
Values may be sent and summed in bfloat16 or wider, within the bound.
A program may use at most 128 MiB of HBM per device.

```python
import math
import jax
import jax.numpy as jnp
from jax import lax

W = 8
L = 3000
F = 512
F0 = 6
LAGS = 2048
BAND = 512
K = 16
CH_TOTAL = 512


def draw_offsets(key, part):
    stride = BAND // K
    index = jnp.arange(K, dtype=jnp.int32)
    base = index * stride + 1
    jitter = jax.random.randint(key, (K,), 0, stride, dtype=jnp.int32)
    jitter = jnp.where(index == K - 1, stride - 2, jitter)
    return (base + jitter).astype(jnp.int32)


def place_ends(entries, own_key, low, largest):
    longest = entries.shape.index(max(entries.shape))
    spots = []
    for shift in (0, 1):
        where = [jax.random.randint(jax.random.fold_in(own_key, axis), (), 0, length) for axis, length in enumerate(entries.shape)]
        where[longest] = (where[longest] + shift) % entries.shape[longest]
        spots.append(tuple(where))
    return entries.at[spots[0]].set(low).at[spots[1]].set(largest)


def shard_levels(rng, dims, cuts, low, high):
    level = 1.0
    for dim, shards_of in cuts:
        steps = jax.random.uniform(jax.random.fold_in(jax.random.fold_in(rng, 6), dim), (shards_of,), jnp.float32, low / len(cuts), high / len(cuts))
        level = level * jnp.repeat(jnp.exp(steps), dims[dim] // shards_of).reshape((-1,) + (1,) * (len(dims) - 1 - dim))
    return level


def normal_values(rng, shape, deviation, bound, shards=(), kind=jnp.bfloat16):
    level = shard_levels(rng, shape, shards, -0.22, 0.18) if shards else 1.0
    drawn = jax.random.normal(rng, shape, jnp.float32) * deviation * level
    return jnp.minimum(jnp.maximum(drawn, -bound), bound).astype(kind)


def setup_inputs(seed: int = 0, part: int = 0) -> dict:
    streams_of = jax.random.split(jax.random.key(seed), 4)
    part_keys = jax.random.split(jax.random.fold_in(streams_of[3], part), 4)
    return {
        "records": normal_values(part_keys[0], (CH_TOTAL, W, L), 1.0, 6.0, ((0, 16),)),
        "live_mask": place_ends((jax.random.randint(part_keys[1], (CH_TOTAL,), 0, 10) < 9).astype(jnp.int32), jax.random.fold_in(part_keys[1], 1), 0, 1),
        "offsets": draw_offsets(jax.random.fold_in(streams_of[3], 71), part),
    }


def forward_table(length):
    samples = jnp.arange(length, dtype=jnp.int32)
    freqs = F0 + jnp.arange(F, dtype=jnp.int32)
    phase = jnp.mod(samples[:, None] * freqs[None, :], length).astype(jnp.float32)
    angle = 2.0 * math.pi / length * phase
    return jnp.concatenate([jnp.cos(angle), -jnp.sin(angle)], axis=1).astype(jnp.bfloat16)

def inverse_table(length):
    freqs = F0 + jnp.arange(F, dtype=jnp.int32)
    shifts = jnp.arange(LAGS, dtype=jnp.int32) - LAGS // 2
    phase = jnp.mod(freqs[:, None] * shifts[None, :], length).astype(jnp.float32)
    angle = 2.0 * math.pi / length * phase
    return jnp.concatenate([jnp.cos(angle), -jnp.sin(angle)], axis=0).astype(jnp.bfloat16)

def whiten(records, live_mask):
    count, windows, length = records.shape
    table = forward_table(length)
    spectrum = jnp.dot(records.reshape(count * windows, length), table, preferred_element_type=jnp.float32)
    power = lax.optimization_barrier(jnp.mean(spectrum * spectrum, axis=1, keepdims=True))
    gain = jnp.repeat(live_mask.astype(jnp.float32), windows)[:, None]
    white = spectrum * (gain * lax.rsqrt(power + 1e-06))
    return white.astype(jnp.bfloat16).reshape(count, windows, 2, spectrum.shape[1] // 2)

def stacked_cross(local_spec, extended, offsets):
    row_count, windows, paired, bin_count = local_spec.shape
    first = local_spec.astype(jnp.float32)

    def single(offset_value):
        partner = lax.dynamic_slice_in_dim(extended, offset_value, row_count, 0).astype(jnp.float32)
        real_part = lax.optimization_barrier(jnp.sum(first[:, :, 0] * partner[:, :, 0] + first[:, :, 1] * partner[:, :, 1], axis=1))
        imag_part = lax.optimization_barrier(jnp.sum(first[:, :, 1] * partner[:, :, 0] - first[:, :, 0] * partner[:, :, 1], axis=1))
        return jnp.stack([real_part, imag_part], axis=1) / float(windows)

    def grouped(group):
        return jax.vmap(single)(group)
    result = lax.map(grouped, offsets.reshape(-1, 8))
    result = result.reshape(offsets.shape[0], row_count, 2, bin_count)
    return jnp.transpose(result, (1, 0, 2, 3)).astype(jnp.bfloat16)

def lag_transform(cross, length):
    count, pairs, paired, bin_count = cross.shape
    table = inverse_table(length)
    result = jnp.dot(cross.reshape(count * pairs, 2 * bin_count), table, preferred_element_type=jnp.float32)
    result = result * (1.0 / math.sqrt(bin_count))
    return result.reshape(count, pairs, table.shape[1]).astype(jnp.bfloat16)

def reference(records, live_mask, offsets):
    spectra = whiten(records, live_mask)
    padding = jnp.zeros((BAND,) + spectra.shape[1:], jnp.bfloat16)
    extended = jnp.concatenate([spectra, padding], axis=0)
    cross = stacked_cross(spectra, extended, offsets)
    return lag_transform(cross, records.shape[2])
```

```python
import functools
import math

import jax
import jax.numpy as jnp
import numpy as np
from jax import lax
from jax.experimental import pallas as pl
from jax.experimental.pallas import tpu as pltpu
from jax.sharding import PartitionSpec as P

F = 512
F0 = 6
LAGS = 2048
LANES = 128


def forward_table(length):
    samples = np.arange(length, dtype=np.int64)
    freqs = F0 + np.arange(F, dtype=np.int64)
    phase = np.mod(samples[:, None] * freqs[None, :], length)
    angle = 2.0 * math.pi / length * phase
    return np.concatenate([np.cos(angle), -np.sin(angle)], axis=1).astype(np.float32).astype(jnp.bfloat16)


def inverse_table(length):
    freqs = F0 + np.arange(F, dtype=np.int64)
    shifts = np.arange(LAGS, dtype=np.int64) - LAGS // 2
    phase = np.mod(freqs[:, None] * shifts[None, :], length)
    angle = 2.0 * math.pi / length * phase
    return np.concatenate([np.cos(angle), -np.sin(angle)], axis=0).astype(np.float32).astype(jnp.bfloat16)


def whiten(records, live_mask):
    count, windows, length = records.shape
    spectrum = jnp.dot(
        records.reshape(count * windows, length),
        jnp.asarray(forward_table(length)),
        preferred_element_type=jnp.float32,
    )
    power = jnp.mean(spectrum * spectrum, axis=1, keepdims=True)
    gain = jnp.repeat(live_mask.astype(jnp.float32), windows)[:, None]
    white = spectrum * (gain * lax.rsqrt(power + 1e-06))
    return white.astype(jnp.bfloat16)


def cross_kernel(windows, offsets_ref, all_ref, cross_ref, own, swapped):
    total = all_ref.shape[0]
    count = own.shape[0]
    pairs = offsets_ref.shape[0]
    first = lax.axis_index("chan") * count
    low = lax.broadcasted_iota(jnp.int32, (8, LANES), 0) < 4

    def prepare(c, carry):
        value = all_ref[first + c].astype(jnp.float32)
        own[c] = value
        for w in range(windows):
            swapped[c, w * 8 : w * 8 + 8] = pltpu.roll(value[w * 8 : w * 8 + 8], 4, 0)
        return carry

    lax.fori_loop(0, count, prepare, 0)

    def channel(c, carry):
        mine = own[c]
        turned = swapped[c]
        for k in range(pairs):
            place = first + c + offsets_ref[k]
            keep = jnp.where(place < total, 1.0 / windows, 0.0)
            partner = all_ref[jnp.minimum(place, total - 1)].astype(jnp.float32)
            straight = mine[:8] * partner[:8]
            twisted = turned[:8] * partner[:8]
            for w in range(1, windows):
                rows = slice(w * 8, w * 8 + 8)
                straight += mine[rows] * partner[rows]
                twisted += turned[rows] * partner[rows]
            joined = jnp.where(
                low,
                straight + pltpu.roll(straight, 4, 0),
                pltpu.roll(twisted, 4, 0) - twisted,
            )
            cross_ref[c, k] = joined * keep
        return carry

    lax.fori_loop(0, count, channel, 0)


def shards(records, live_mask, offsets):
    count, windows, length = records.shape
    pairs = offsets.shape[0]
    spectra = whiten(records, live_mask).reshape(count, windows * 8, LANES)
    gathered = lax.all_gather(spectra, "chan", axis=0, tiled=True)
    cross = pl.pallas_call(
        functools.partial(cross_kernel, windows),
        out_shape=jax.ShapeDtypeStruct((count, pairs, 8, LANES), jnp.float32),
        in_specs=[
            pl.BlockSpec(memory_space=pltpu.SMEM),
            pl.BlockSpec(memory_space=pltpu.VMEM),
        ],
        out_specs=pl.BlockSpec(memory_space=pltpu.VMEM),
        scratch_shapes=[
            pltpu.VMEM((count, windows * 8, LANES), jnp.float32),
            pltpu.VMEM((count, windows * 8, LANES), jnp.float32),
        ],
        compiler_params=pltpu.CompilerParams(vmem_limit_bytes=40 * 1024 * 1024),
    )(offsets, gathered)
    cross = cross.astype(jnp.bfloat16).reshape(count * pairs, 8 * LANES)
    result = jnp.dot(cross, jnp.asarray(inverse_table(length)), preferred_element_type=jnp.float32)
    result = result * (1.0 / math.sqrt(F))
    return result.reshape(count, pairs, LAGS).astype(jnp.bfloat16)


def solution(mesh):
    in_specs = (P(("day", "chan"), None, None), P(("day", "chan")), P())
    out_specs = P(("day", "chan"), None, None)
    return jax.shard_map(shards, mesh=mesh, in_specs=in_specs, out_specs=out_specs, check_vma=False)
```

```python
import functools
import math

import jax
import jax.numpy as jnp
import numpy as np
from jax import lax
from jax.experimental import pallas as pl
from jax.experimental.pallas import tpu as pltpu
from jax.sharding import PartitionSpec as P

F = 512
F0 = 6
LAGS = 2048
LANES = 128
BAND = 512
PIECES = 2
LAYER_CHIPS = 4


def forward_table(length):
    samples = np.arange(length, dtype=np.int64)
    freqs = F0 + np.arange(F, dtype=np.int64)
    phase = np.mod(samples[:, None] * freqs[None, :], length)
    angle = 2.0 * math.pi / length * phase
    return np.concatenate([np.cos(angle), -np.sin(angle)], axis=1).astype(np.float32).astype(jnp.bfloat16)


def inverse_table(length):
    freqs = F0 + np.arange(F, dtype=np.int64)
    shifts = np.arange(LAGS, dtype=np.int64) - LAGS // 2
    phase = np.mod(freqs[:, None] * shifts[None, :], length)
    angle = 2.0 * math.pi / length * phase
    return np.concatenate([np.cos(angle), -np.sin(angle)], axis=0).astype(np.float32).astype(jnp.bfloat16)


def whiten(records, live_mask):
    count, windows, length = records.shape
    spectrum = jnp.dot(
        records.reshape(count * windows, length),
        jnp.asarray(forward_table(length)),
        preferred_element_type=jnp.float32,
    )
    power = jnp.mean(spectrum * spectrum, axis=1, keepdims=True)
    gain = jnp.repeat(live_mask.astype(jnp.float32), windows)[:, None]
    white = spectrum * (gain * lax.rsqrt(power + 1e-06))
    return white.astype(jnp.bfloat16)


def reach_kernel(shape, offsets_ref, white_ref, cross_ref, held, ext, own, swapped,
                 z_send, z_recv, c_send, c_recv, y_send, y_recv, d_send, d_recv):
    layers, columns, depth, pieces, windows = shape
    count, slab = white_ref.shape[0], white_ref.shape[1]
    pairs = offsets_ref.shape[0]
    wide = 2 * columns
    total = layers * wide * count
    me = lax.axis_index("chan")
    z, q = me // wide, me % wide
    y, c = q // 2, q % 2
    sibling = me + 1 - 2 * c
    sib_q = q + 1 - 2 * c
    mate = me + 2 - 4 * y
    mate_q = q + 2 - 4 * y
    far_q = sib_q + 2 - 4 * y
    step = count // pieces

    barrier = pltpu.get_barrier_semaphore()

    def greet(device):
        pl.semaphore_signal(barrier, inc=1, device_id={"chan": device}, device_id_type=pl.DeviceIdType.MESH)

    greet(sibling)
    if columns == 2:
        greet(mate)

    @pl.when(z >= 1)
    def _():
        greet(me - wide)

    @pl.when(z < layers - 1)
    def _():
        greet(me + wide)

    above = jnp.minimum(layers - 1 - z, 1)
    pl.semaphore_wait(barrier, columns + jnp.minimum(z, 1) + above)

    def rows(p):
        return pl.ds(p * step, step)

    def mine(dz, p):
        return white_ref.at[rows(p)] if dz == 0 else held.at[dz * wide + q, rows(p)]

    def copy(source, slot, p, send, recv, device):
        return pltpu.make_async_remote_copy(
            src_ref=source,
            dst_ref=held.at[slot, rows(p)],
            send_sem=send,
            recv_sem=recv,
            device_id={"chan": device},
            device_id_type=pl.DeviceIdType.MESH,
        )

    def down(dz, p):
        return copy(mine(dz, p), (dz + 1) * wide + q, p, z_send.at[dz, p], z_recv.at[dz + 1, p], me - wide)

    def from_above(dz, p):
        return copy(mine(dz, p), dz * wide + q, p, z_send.at[dz, p], z_recv.at[dz, p], me)

    def across(dz, p, slot):
        return copy(mine(dz, p), slot, p, c_send.at[dz, p], c_recv.at[dz, p], sibling)

    def over(dz, p, slot):
        return copy(mine(dz, p), slot, p, y_send.at[dz, p], y_recv.at[dz, p], mate)

    def onward(dz, p, slot):
        return copy(held.at[dz * wide + mate_q, rows(p)], slot, p, d_send.at[dz, p], d_recv.at[dz, p], sibling)

    def both(*conditions):
        joined = conditions[0]
        for condition in conditions[1:]:
            joined = jnp.logical_and(joined, condition)
        return joined

    def exists(dz):
        return z + dz < layers

    def sends(dz):
        for p in range(pieces):
            if dz > 0:
                @pl.when(exists(dz))
                def _():
                    from_above(dz, p).wait_recv()
            if dz < depth:
                @pl.when(both(exists(dz), z >= 1))
                def _():
                    down(dz, p).start()
            if columns == 2:
                @pl.when(both(exists(dz), y == 1) if dz == 0 else exists(dz))
                def _():
                    over(dz, p, dz * wide + q).start()
            @pl.when(both(exists(dz), c == 1) if dz == 0 else exists(dz))
            def _():
                across(dz, p, dz * wide + q).start()

    def passes(dz):
        if columns == 2:
            for p in range(pieces):
                @pl.when(both(exists(dz), y == 0) if dz == 0 else exists(dz))
                def _():
                    over(dz, p, dz * wide + mate_q).wait_recv()
                    onward(dz, p, dz * wide + mate_q).start()

    def arrives(dz):
        for p in range(pieces):
            @pl.when(both(exists(dz), c == 0) if dz == 0 else exists(dz))
            def _():
                across(dz, p, dz * wide + sib_q).wait_recv()
            if columns == 2:
                @pl.when(both(exists(dz), y == 0) if dz == 0 else exists(dz))
                def _():
                    onward(dz, p, dz * wide + far_q).wait_recv()

    def finishes(dz):
        for p in range(pieces):
            if dz < depth:
                @pl.when(both(exists(dz), z >= 1))
                def _():
                    down(dz, p).wait_send()
            if columns == 2:
                @pl.when(both(exists(dz), y == 1) if dz == 0 else exists(dz))
                def _():
                    over(dz, p, dz * wide + q).wait_send()
                @pl.when(both(exists(dz), y == 0) if dz == 0 else exists(dz))
                def _():
                    onward(dz, p, dz * wide + mate_q).wait_send()
            @pl.when(both(exists(dz), c == 1) if dz == 0 else exists(dz))
            def _():
                across(dz, p, dz * wide + q).wait_send()

    low = lax.broadcasted_iota(jnp.int32, (8, LANES), 0) < 4

    def prepare(i, carry):
        raw = white_ref[i]
        value = raw.astype(jnp.float32)
        own[i] = value
        ext[q * count + i] = raw
        for w in range(windows):
            swapped[i, w * 8 : w * 8 + 8] = pltpu.roll(value[w * 8 : w * 8 + 8], 4, 0)
        return carry

    def settle(dz):
        def one(l):
            def fill(i, carry):
                ext[(dz * wide + l) * count + i] = held[dz * wide + l, i]
                return carry
            lax.fori_loop(0, count, fill, 0, unroll=4)

        def none(i, carry):
            ext[dz * wide * count + i] = jnp.zeros((slab, LANES), jnp.bfloat16)
            return carry

        if dz == 0:
            for l in range(1, wide):
                @pl.when(q < l)
                def _():
                    one(l)
        else:
            @pl.when(exists(dz))
            def _():
                for l in range(wide):
                    one(l)

            @pl.when(jnp.logical_not(exists(dz)))
            def _():
                lax.fori_loop(0, wide * count, none, 0, unroll=4)

    def reached(dz):
        if dz < 0:
            return 0
        if dz == depth:
            return pairs
        return jnp.clip((dz + 1) * wide - q - 1, 0, pairs)

    def multiply(dz):
        def pair(k, carry):
            shift = offsets_ref[k]

            def channel(i, inner):
                place = me * count + i + shift
                keep = jnp.where(place < total, 1.0 / windows, 0.0)
                near = jnp.minimum(q * count + i + shift, ext.shape[0] - 1)
                partner = ext[near].astype(jnp.float32)
                straight = own[i, :8] * partner[:8]
                twisted = swapped[i, :8] * partner[:8]
                for w in range(1, windows):
                    part = slice(w * 8, w * 8 + 8)
                    straight += own[i, part] * partner[part]
                    twisted += swapped[i, part] * partner[part]
                joined = jnp.where(
                    low,
                    straight + pltpu.roll(straight, 4, 0),
                    pltpu.roll(twisted, 4, 0) - twisted,
                )
                cross_ref[i, k] = joined * keep
                return inner

            return lax.fori_loop(0, count, channel, carry, unroll=4)

        lax.fori_loop(reached(dz - 1), reached(dz), pair, 0)

    sends(0)
    lax.fori_loop(0, count, prepare, 0)
    for dz in range(depth + 1):
        if dz < depth:
            sends(dz + 1)
        passes(dz)
        arrives(dz)
        settle(dz)
        multiply(dz)
    for dz in range(depth + 1):
        finishes(dz)


def shards(columns, records, live_mask, offsets):
    count, windows, length = records.shape
    pairs = offsets.shape[0]
    wide = 2 * columns
    layers = lax.axis_size("chan") // wide
    reach = (BAND + count - 2) // count
    depth = min(layers - 1, (wide - 1 + reach) // wide)
    pieces = PIECES
    spectra = whiten(records, live_mask).reshape(count, windows * 8, LANES)
    slots = (depth + 1) * wide
    cross = pl.pallas_call(
        functools.partial(reach_kernel, (layers, columns, depth, pieces, windows)),
        out_shape=jax.ShapeDtypeStruct((count, pairs, 8, LANES), jnp.float32),
        in_specs=[
            pl.BlockSpec(memory_space=pltpu.SMEM),
            pl.BlockSpec(memory_space=pltpu.VMEM),
        ],
        out_specs=pl.BlockSpec(memory_space=pltpu.VMEM),
        scratch_shapes=[
            pltpu.VMEM((slots, count, windows * 8, LANES), jnp.bfloat16),
            pltpu.VMEM((slots * count, windows * 8, LANES), jnp.bfloat16),
            pltpu.VMEM((count, windows * 8, LANES), jnp.float32),
            pltpu.VMEM((count, windows * 8, LANES), jnp.float32),
        ]
        + [pltpu.SemaphoreType.DMA((depth + 1, pieces))] * 8,
        compiler_params=pltpu.CompilerParams(
            vmem_limit_bytes=40 * 1024 * 1024, collective_id=0, has_side_effects=True
        ),
    )(offsets, spectra)
    cross = cross.astype(jnp.bfloat16).reshape(count * pairs, 8 * LANES)
    result = jnp.dot(cross, jnp.asarray(inverse_table(length)), preferred_element_type=jnp.float32)
    result = result * (1.0 / math.sqrt(F))
    return result.reshape(count, pairs, LAGS).astype(jnp.bfloat16)


def solution(mesh):
    in_specs = (P(("day", "chan"), None, None), P(("day", "chan")), P())
    out_specs = P(("day", "chan"), None, None)
    columns = max(1, LAYER_CHIPS // mesh.shape["day"])
    body = functools.partial(shards, columns)
    return jax.shard_map(body, mesh=mesh, in_specs=in_specs, out_specs=out_specs, check_vma=False)
```

```python
import functools
import math

import jax
import jax.numpy as jnp
import numpy as np
from jax import lax
from jax.experimental import pallas as pl
from jax.experimental.pallas import tpu as pltpu
from jax.sharding import PartitionSpec as P

F = 512
F0 = 6
LAGS = 2048
LANES = 128
BAND = 512
PIECES = 2
LAYER_CHIPS = 4


def forward_table(length):
    samples = np.arange(length, dtype=np.int64)
    freqs = F0 + np.arange(F, dtype=np.int64)
    phase = np.mod(samples[:, None] * freqs[None, :], length)
    angle = 2.0 * math.pi / length * phase
    return np.concatenate([np.cos(angle), -np.sin(angle)], axis=1).astype(np.float32).astype(jnp.bfloat16)


def inverse_table(length):
    freqs = F0 + np.arange(F, dtype=np.int64)
    shifts = np.arange(LAGS, dtype=np.int64) - LAGS // 2
    phase = np.mod(freqs[:, None] * shifts[None, :], length)
    angle = 2.0 * math.pi / length * phase
    return np.concatenate([np.cos(angle), -np.sin(angle)], axis=0).astype(np.float32).astype(jnp.bfloat16)


def whiten(records, live_mask):
    count, windows, length = records.shape
    spectrum = jnp.dot(
        records.reshape(count * windows, length),
        jnp.asarray(forward_table(length)),
        preferred_element_type=jnp.float32,
    )
    power = jnp.mean(spectrum * spectrum, axis=1, keepdims=True)
    gain = jnp.repeat(live_mask.astype(jnp.float32), windows)[:, None]
    white = spectrum * (gain * lax.rsqrt(power + 1e-06))
    return white.astype(jnp.bfloat16)


def reach_kernel(shape, offsets_ref, white_ref, cross_ref, held, ext, own, swapped,
                 z_send, z_recv, c_send, c_recv, y_send, y_recv, d_send, d_recv, e_send):
    layers, columns, depth, pieces, windows = shape
    count, slab = white_ref.shape[0], white_ref.shape[1]
    pairs = offsets_ref.shape[0]
    wide = 2 * columns
    total = layers * wide * count
    me = lax.axis_index("chan")
    z, q = me // wide, me % wide
    y, c = q // 2, q % 2
    sibling = me + 1 - 2 * c
    sib_q = q + 1 - 2 * c
    mate = me + 2 - 4 * y
    mate_q = q + 2 - 4 * y
    far_q = sib_q + 2 - 4 * y
    step = count // pieces

    barrier = pltpu.get_barrier_semaphore()

    def greet(device):
        pl.semaphore_signal(barrier, inc=1, device_id={"chan": device}, device_id_type=pl.DeviceIdType.MESH)

    greet(sibling)
    if columns == 2:
        greet(mate)

    @pl.when(z >= 1)
    def _():
        greet(me - wide)

    @pl.when(z < layers - 1)
    def _():
        greet(me + wide)

    above = jnp.minimum(layers - 1 - z, 1)
    pl.semaphore_wait(barrier, columns + jnp.minimum(z, 1) + above)

    def rows(p):
        return pl.ds(p * step, step)

    def mine(dz, p):
        return white_ref.at[rows(p)] if dz == 0 else held.at[dz * wide + q, rows(p)]

    def copy(source, slot, p, send, recv, device):
        return pltpu.make_async_remote_copy(
            src_ref=source,
            dst_ref=held.at[slot, rows(p)],
            send_sem=send,
            recv_sem=recv,
            device_id={"chan": device},
            device_id_type=pl.DeviceIdType.MESH,
        )

    def down(dz, p):
        return copy(mine(dz, p), (dz + 1) * wide + q, p, z_send.at[dz, p], z_recv.at[dz + 1, p], me - wide)

    def from_above(dz, p):
        return copy(mine(dz, p), dz * wide + q, p, z_send.at[dz, p], z_recv.at[dz, p], me)

    def across(dz, p, slot):
        return copy(mine(dz, p), slot, p, c_send.at[dz, p], c_recv.at[dz, p], sibling)

    def over(dz, p, slot):
        return copy(mine(dz, p), slot, p, y_send.at[dz, p], y_recv.at[dz, p], mate)

    def onward(dz, p, slot):
        return copy(held.at[dz * wide + mate_q, rows(p)], slot, p, d_send.at[dz, p], d_recv.at[dz, p], sibling)

    def both(*conditions):
        joined = conditions[0]
        for condition in conditions[1:]:
            joined = jnp.logical_and(joined, condition)
        return joined

    def exists(dz):
        return z + dz < layers

    def last(dz):
        return z + dz == layers - 1

    detours = columns == 2 and depth == layers - 1

    def detoured(dz, p):
        return detours and dz > 0 and p >= pieces - pieces // 2

    def goes_over(dz, p):
        if dz == 0:
            return both(exists(dz), y == 1)
        if detoured(dz, p):
            return both(exists(dz), jnp.logical_not(both(last(dz), y == 1)))
        return exists(dz)

    def extra(dz, p):
        return copy(held.at[dz * wide + mate_q, rows(p)], (dz + 1) * wide + mate_q, p,
                    e_send.at[dz, p], y_recv.at[dz + 1, p], me - wide)

    def goes_extra(dz):
        return both(last(dz), y == 0, z >= 1)

    def sends(dz):
        for p in range(pieces):
            if dz > 0:
                @pl.when(exists(dz))
                def _():
                    from_above(dz, p).wait_recv()
            if dz < depth:
                @pl.when(both(exists(dz), z >= 1))
                def _():
                    down(dz, p).start()
            if columns == 2:
                @pl.when(goes_over(dz, p))
                def _():
                    over(dz, p, dz * wide + q).start()
            @pl.when(both(exists(dz), c == 1) if dz == 0 else exists(dz))
            def _():
                across(dz, p, dz * wide + q).start()

    def passes(dz):
        if columns == 2:
            for p in range(pieces):
                @pl.when(both(exists(dz), y == 0) if dz == 0 else exists(dz))
                def _():
                    over(dz, p, dz * wide + mate_q).wait_recv()
                    onward(dz, p, dz * wide + mate_q).start()
                if dz < depth and detoured(dz + 1, p):
                    @pl.when(goes_extra(dz))
                    def _():
                        extra(dz, p).start()

    def arrives(dz):
        for p in range(pieces):
            @pl.when(both(exists(dz), c == 0) if dz == 0 else exists(dz))
            def _():
                across(dz, p, dz * wide + sib_q).wait_recv()
            if columns == 2:
                @pl.when(both(exists(dz), y == 0) if dz == 0 else exists(dz))
                def _():
                    onward(dz, p, dz * wide + far_q).wait_recv()

    def finishes(dz):
        for p in range(pieces):
            if dz < depth:
                @pl.when(both(exists(dz), z >= 1))
                def _():
                    down(dz, p).wait_send()
            if columns == 2:
                @pl.when(goes_over(dz, p))
                def _():
                    over(dz, p, dz * wide + q).wait_send()
                if dz < depth and detoured(dz + 1, p):
                    @pl.when(goes_extra(dz))
                    def _():
                        extra(dz, p).wait_send()
                @pl.when(both(exists(dz), y == 0) if dz == 0 else exists(dz))
                def _():
                    onward(dz, p, dz * wide + mate_q).wait_send()
            @pl.when(both(exists(dz), c == 1) if dz == 0 else exists(dz))
            def _():
                across(dz, p, dz * wide + q).wait_send()

    low = lax.broadcasted_iota(jnp.int32, (8, LANES), 0) < 4

    def prepare(i, carry):
        raw = white_ref[i]
        value = raw.astype(jnp.float32)
        own[i] = value
        ext[q * count + i] = raw
        for w in range(windows):
            swapped[i, w * 8 : w * 8 + 8] = pltpu.roll(value[w * 8 : w * 8 + 8], 4, 0)
        return carry

    def settle(dz):
        def one(l):
            def fill(i, carry):
                ext[(dz * wide + l) * count + i] = held[dz * wide + l, i]
                return carry
            lax.fori_loop(0, count, fill, 0, unroll=4)

        def none(i, carry):
            ext[dz * wide * count + i] = jnp.zeros((slab, LANES), jnp.bfloat16)
            return carry

        if dz == 0:
            for l in range(1, wide):
                @pl.when(q < l)
                def _():
                    one(l)
        else:
            @pl.when(exists(dz))
            def _():
                for l in range(wide):
                    one(l)

            @pl.when(jnp.logical_not(exists(dz)))
            def _():
                lax.fori_loop(0, wide * count, none, 0, unroll=4)

    def reached(dz):
        if dz < 0:
            return 0
        if dz == depth:
            return pairs
        return jnp.clip((dz + 1) * wide - q - 1, 0, pairs)

    def multiply(dz):
        def pair(k, carry):
            shift = offsets_ref[k]

            def channel(i, inner):
                place = me * count + i + shift
                keep = jnp.where(place < total, 1.0 / windows, 0.0)
                near = jnp.minimum(q * count + i + shift, ext.shape[0] - 1)
                partner = ext[near].astype(jnp.float32)
                straight = own[i, :8] * partner[:8]
                twisted = swapped[i, :8] * partner[:8]
                for w in range(1, windows):
                    part = slice(w * 8, w * 8 + 8)
                    straight += own[i, part] * partner[part]
                    twisted += swapped[i, part] * partner[part]
                joined = jnp.where(
                    low,
                    straight + pltpu.roll(straight, 4, 0),
                    pltpu.roll(twisted, 4, 0) - twisted,
                )
                cross_ref[i, k] = joined * keep
                return inner

            return lax.fori_loop(0, count, channel, carry, unroll=4)

        lax.fori_loop(reached(dz - 1), reached(dz), pair, 0)

    sends(0)
    lax.fori_loop(0, count, prepare, 0)
    for dz in range(depth + 1):
        if dz < depth:
            sends(dz + 1)
        passes(dz)
        arrives(dz)
        settle(dz)
        multiply(dz)
    for dz in range(depth + 1):
        finishes(dz)


def shards(columns, records, live_mask, offsets):
    count, windows, length = records.shape
    pairs = offsets.shape[0]
    wide = 2 * columns
    layers = lax.axis_size("chan") // wide
    reach = (BAND + count - 2) // count
    depth = min(layers - 1, (wide - 1 + reach) // wide)
    pieces = PIECES
    spectra = whiten(records, live_mask).reshape(count, windows * 8, LANES)
    slots = (depth + 1) * wide
    cross = pl.pallas_call(
        functools.partial(reach_kernel, (layers, columns, depth, pieces, windows)),
        out_shape=jax.ShapeDtypeStruct((count, pairs, 8, LANES), jnp.float32),
        in_specs=[
            pl.BlockSpec(memory_space=pltpu.SMEM),
            pl.BlockSpec(memory_space=pltpu.VMEM),
        ],
        out_specs=pl.BlockSpec(memory_space=pltpu.VMEM),
        scratch_shapes=[
            pltpu.VMEM((slots, count, windows * 8, LANES), jnp.bfloat16),
            pltpu.VMEM((slots * count, windows * 8, LANES), jnp.bfloat16),
            pltpu.VMEM((count, windows * 8, LANES), jnp.float32),
            pltpu.VMEM((count, windows * 8, LANES), jnp.float32),
        ]
        + [pltpu.SemaphoreType.DMA((depth + 1, pieces))] * 9,
        compiler_params=pltpu.CompilerParams(
            vmem_limit_bytes=40 * 1024 * 1024, collective_id=0, has_side_effects=True
        ),
    )(offsets, spectra)
    cross = cross.astype(jnp.bfloat16).reshape(count * pairs, 8 * LANES)
    result = jnp.dot(cross, jnp.asarray(inverse_table(length)), preferred_element_type=jnp.float32)
    result = result * (1.0 / math.sqrt(F))
    return result.reshape(count, pairs, LAGS).astype(jnp.bfloat16)


def solution(mesh):
    in_specs = (P(("day", "chan"), None, None), P(("day", "chan")), P())
    out_specs = P(("day", "chan"), None, None)
    columns = max(1, LAYER_CHIPS // mesh.shape["day"])
    body = functools.partial(shards, columns)
    return jax.shard_map(body, mesh=mesh, in_specs=in_specs, out_specs=out_specs, check_vma=False)
```

```python
import functools
import math

import jax
import jax.numpy as jnp
import numpy as np
from jax import lax
from jax.experimental import pallas as pl
from jax.experimental.pallas import tpu as pltpu
from jax.sharding import PartitionSpec as P

F = 512
F0 = 6
LAGS = 2048
LANES = 128
BAND = 512
PIECES = 2
LAYER_CHIPS = 4


def forward_table(length):
    samples = np.arange(length, dtype=np.int64)
    freqs = F0 + np.arange(F, dtype=np.int64)
    phase = np.mod(samples[:, None] * freqs[None, :], length)
    angle = 2.0 * math.pi / length * phase
    return np.concatenate([np.cos(angle), -np.sin(angle)], axis=1).astype(np.float32).astype(jnp.bfloat16)


def inverse_table(length):
    freqs = F0 + np.arange(F, dtype=np.int64)
    shifts = np.arange(LAGS, dtype=np.int64) - LAGS // 2
    phase = np.mod(freqs[:, None] * shifts[None, :], length)
    angle = 2.0 * math.pi / length * phase
    return np.concatenate([np.cos(angle), -np.sin(angle)], axis=0).astype(np.float32).astype(jnp.bfloat16)


def whiten(records, live_mask):
    count, windows, length = records.shape
    spectrum = jnp.dot(
        records.reshape(count * windows, length),
        jnp.asarray(forward_table(length)),
        preferred_element_type=jnp.float32,
    )
    power = jnp.mean(spectrum * spectrum, axis=1, keepdims=True)
    gain = jnp.repeat(live_mask.astype(jnp.float32), windows)[:, None]
    white = spectrum * (gain * lax.rsqrt(power + 1e-06))
    return white.astype(jnp.bfloat16)


def reach_kernel(shape, offsets_ref, white_ref, cross_ref, held, ext, own, swapped, made, back,
                 z_send, z_recv, c_send, c_recv, y_send, y_recv, d_send, d_recv, r_send, r_recv):
    layers, columns, depth, pieces, windows, fold = shape
    count, slab = white_ref.shape[0], white_ref.shape[1]
    pairs = offsets_ref.shape[0]
    wide = 2 * columns
    total = layers * wide * count
    me = lax.axis_index("chan")
    z, q = me // wide, me % wide
    y, c = q // 2, q % 2
    sibling = me + 1 - 2 * c
    sib_q = q + 1 - 2 * c
    mate = me + 2 - 4 * y
    mate_q = q + 2 - 4 * y
    far_q = sib_q + 2 - 4 * y
    step = count // pieces
    top, lifted = layers - 1, depth + 1

    barrier = pltpu.get_barrier_semaphore()

    def greet(device):
        pl.semaphore_signal(barrier, inc=1, device_id={"chan": device}, device_id_type=pl.DeviceIdType.MESH)

    greet(sibling)
    if columns == 2:
        greet(mate)

    @pl.when(z >= 1)
    def _():
        greet(me - wide)

    @pl.when(z < layers - 1)
    def _():
        greet(me + wide)

    below, above = jnp.minimum(z, 1), jnp.minimum(top - z, 1)
    peers = columns + below + above
    if fold:
        @pl.when(z == 0)
        def _():
            for i in range(wide):
                greet(top * wide + i)

        @pl.when(z == top)
        def _():
            for i in range(wide):
                greet(jnp.int32(i))

        peers = peers + wide * (2 - below - above)
    pl.semaphore_wait(barrier, peers)

    def rows(p):
        return pl.ds(p * step, step)

    def mine(dz, p):
        return white_ref.at[rows(p)] if dz == 0 else held.at[dz * wide + q, rows(p)]

    def copy(source, slot, p, send, recv, device):
        return pltpu.make_async_remote_copy(
            src_ref=source,
            dst_ref=held.at[slot, rows(p)],
            send_sem=send,
            recv_sem=recv,
            device_id={"chan": device},
            device_id_type=pl.DeviceIdType.MESH,
        )

    def down(dz, p):
        return copy(mine(dz, p), (dz + 1) * wide + q, p, z_send.at[dz, p], z_recv.at[dz + 1, p], me - wide)

    def from_above(dz, p):
        return copy(mine(dz, p), dz * wide + q, p, z_send.at[dz, p], z_recv.at[dz, p], me)

    def across(dz, p, slot):
        return copy(mine(dz, p), slot, p, c_send.at[dz, p], c_recv.at[dz, p], sibling)

    def over(dz, p, slot):
        return copy(mine(dz, p), slot, p, y_send.at[dz, p], y_recv.at[dz, p], mate)

    def onward(dz, p, slot):
        return copy(held.at[dz * wide + mate_q, rows(p)], slot, p, d_send.at[dz, p], d_recv.at[dz, p], sibling)

    def both(*conditions):
        joined = conditions[0]
        for condition in conditions[1:]:
            joined = jnp.logical_and(joined, condition)
        return joined

    def exists(dz):
        return z + dz < layers

    def goes(dz, at_start, at_end):
        if dz == lifted:
            return z == top
        if dz == 0:
            return at_start
        if fold and dz == depth:
            return both(exists(dz), at_end)
        return exists(dz)

    def z_tx(dz):
        if fold and dz + 1 == depth:
            return both(exists(dz), z >= 1, jnp.logical_or(z >= 2, q == 0))
        return both(exists(dz), z >= 1)

    def z_rx(dz):
        return goes(dz, None, q == 0)

    def c_tx(dz):
        return goes(dz, c == 1, q == 0)

    def c_rx(dz):
        return goes(dz, c == 0, q == 1)

    def y_tx(dz):
        return goes(dz, y == 1, q == 0)

    def y_rx(dz):
        return goes(dz, y == 0, q == 2)

    def d_rx(dz):
        return goes(dz, y == 0, q == 3)

    def lift(p):
        return copy(white_ref.at[rows(p)], lifted * wide + q, p, z_send.at[lifted, p], z_recv.at[lifted, p],
                    me + top * wide)

    def sends(dz):
        for p in range(pieces):
            if dz > 0:
                @pl.when(z_rx(dz))
                def _():
                    from_above(dz, p).wait_recv()
            if dz < depth:
                @pl.when(z_tx(dz))
                def _():
                    down(dz, p).start()
            if columns == 2:
                @pl.when(y_tx(dz))
                def _():
                    over(dz, p, dz * wide + q).start()
            @pl.when(c_tx(dz))
            def _():
                across(dz, p, dz * wide + q).start()

    def passes(dz):
        if columns == 2:
            for p in range(pieces):
                @pl.when(y_rx(dz))
                def _():
                    over(dz, p, dz * wide + mate_q).wait_recv()
                    onward(dz, p, dz * wide + mate_q).start()

    def arrives(dz):
        for p in range(pieces):
            @pl.when(c_rx(dz))
            def _():
                across(dz, p, dz * wide + sib_q).wait_recv()
            if columns == 2:
                @pl.when(d_rx(dz))
                def _():
                    onward(dz, p, dz * wide + far_q).wait_recv()

    def finishes(dz):
        for p in range(pieces):
            if dz < depth:
                @pl.when(z_tx(dz))
                def _():
                    down(dz, p).wait_send()
            if columns == 2:
                @pl.when(y_tx(dz))
                def _():
                    over(dz, p, dz * wide + q).wait_send()
                @pl.when(y_rx(dz))
                def _():
                    onward(dz, p, dz * wide + mate_q).wait_send()
            @pl.when(c_tx(dz))
            def _():
                across(dz, p, dz * wide + q).wait_send()

    def answer(i):
        return pltpu.make_async_remote_copy(
            src_ref=made.at[i],
            dst_ref=back.at[q],
            send_sem=r_send.at[i],
            recv_sem=r_recv.at[q],
            device_id={"chan": jnp.int32(i)},
            device_id_type=pl.DeviceIdType.MESH,
        )

    def answered(i):
        return pltpu.make_async_remote_copy(
            src_ref=made.at[i],
            dst_ref=back.at[i],
            send_sem=r_send.at[i],
            recv_sem=r_recv.at[i],
            device_id={"chan": me},
            device_id_type=pl.DeviceIdType.MESH,
        )

    low = lax.broadcasted_iota(jnp.int32, (8, LANES), 0) < 4

    def prepare(i, carry):
        raw = white_ref[i]
        value = raw.astype(jnp.float32)
        own[i] = value
        ext[q * count + i] = raw
        for w in range(windows):
            swapped[i, w * 8 : w * 8 + 8] = pltpu.roll(value[w * 8 : w * 8 + 8], 4, 0)
        return carry

    def settle(dz):
        def one(l):
            def fill(i, carry):
                ext[(dz * wide + l) * count + i] = held[dz * wide + l, i]
                return carry
            lax.fori_loop(0, count, fill, 0, unroll=4)

        def none(i, carry):
            ext[dz * wide * count + i] = jnp.zeros((slab, LANES), jnp.bfloat16)
            return carry

        if dz == 0:
            for l in range(1, wide):
                @pl.when(q < l)
                def _():
                    one(l)
        else:
            @pl.when(exists(dz))
            def _():
                for l in range(1 if fold and dz == depth else wide):
                    one(l)

            @pl.when(jnp.logical_not(exists(dz)))
            def _():
                lax.fori_loop(0, wide * count, none, 0, unroll=4)

    def reached(dz):
        if dz < 0:
            return 0
        if dz == depth:
            return pairs
        return jnp.clip((dz + 1) * wide - q - 1, 0, pairs)

    def multiply(dz):
        def pair(k, carry):
            shift = offsets_ref[k]

            def channel(i, inner):
                place = me * count + i + shift
                keep = jnp.where(place < total, 1.0 / windows, 0.0)
                near = jnp.minimum(q * count + i + shift, ext.shape[0] - 1)
                partner = ext[near].astype(jnp.float32)
                straight = own[i, :8] * partner[:8]
                twisted = swapped[i, :8] * partner[:8]
                for w in range(1, windows):
                    part = slice(w * 8, w * 8 + 8)
                    straight += own[i, part] * partner[part]
                    twisted += swapped[i, part] * partner[part]
                joined = jnp.where(
                    low,
                    straight + pltpu.roll(straight, 4, 0),
                    pltpu.roll(twisted, 4, 0) - twisted,
                )
                cross_ref[i, k] = joined * keep
                return inner

            return lax.fori_loop(0, count, channel, carry, unroll=4)

        begin, end = reached(dz - 1), reached(dz)
        if fold and dz == depth:
            @pl.when(z == 0)
            def _():
                lax.fori_loop(begin, begin + 1, pair, 0)

            @pl.when(z > 0)
            def _():
                lax.fori_loop(begin, end, pair, 0)
        else:
            lax.fori_loop(begin, end, pair, 0)

    def reply():
        for i in range(wide):
            shift = offsets_ref[top * wide + q - i]

            def channel(r, carry):
                place = i * count + r + shift
                keep = jnp.where(place < total, 1.0 / windows, 0.0)
                near = jnp.clip(place - top * wide * count, 0, ext.shape[0] - 1)
                partner = ext[near].astype(jnp.float32)
                value = held[lifted * wide + i, r].astype(jnp.float32)
                straight = value[:8] * partner[:8]
                twisted = pltpu.roll(value[:8], 4, 0) * partner[:8]
                for w in range(1, windows):
                    part = slice(w * 8, w * 8 + 8)
                    straight += value[part] * partner[part]
                    twisted += pltpu.roll(value[part], 4, 0) * partner[part]
                joined = jnp.where(
                    low,
                    straight + pltpu.roll(straight, 4, 0),
                    pltpu.roll(twisted, 4, 0) - twisted,
                )
                made[i, r] = (joined * keep).astype(jnp.bfloat16)
                return carry

            lax.fori_loop(0, count, channel, 0, unroll=4)
        for i in range(wide):
            answer(i).start()

    sends(0)
    if fold:
        @pl.when(z == 0)
        def _():
            for p in range(pieces):
                lift(p).start()

    lax.fori_loop(0, count, prepare, 0)
    for dz in range(depth + 1):
        if dz < depth:
            sends(dz + 1)
        if fold and dz == 0:
            sends(lifted)
        passes(dz)
        if fold and dz == 0:
            passes(lifted)
        arrives(dz)
        settle(dz)
        if fold and dz == 0:
            arrives(lifted)

            @pl.when(z == top)
            def _():
                def blank(i, carry):
                    ext[wide * count + i] = jnp.zeros((slab, LANES), jnp.bfloat16)
                    return carry

                lax.fori_loop(0, 2 * count, blank, 0, unroll=4)
                reply()

        multiply(dz)

    if fold:
        @pl.when(z == 0)
        def _():
            def nothing(k, carry):
                for r in range(count):
                    cross_ref[r, k] = jnp.zeros((8, LANES), jnp.float32)
                return carry

            lax.fori_loop(pairs - q, pairs, nothing, 0)
            for i in range(wide):
                answered(i).wait_recv()

                def take(r, carry):
                    cross_ref[r, top * wide - q + i] = back[i, r].astype(jnp.float32)
                    return carry

                lax.fori_loop(0, count, take, 0, unroll=4)
            for p in range(pieces):
                lift(p).wait_send()

        @pl.when(z == top)
        def _():
            for i in range(wide):
                answer(i).wait_send()

        finishes(lifted)
    for dz in range(depth + 1):
        finishes(dz)


def shards(columns, records, live_mask, offsets):
    count, windows, length = records.shape
    pairs = offsets.shape[0]
    wide = 2 * columns
    layers = lax.axis_size("chan") // wide
    reach = (BAND + count - 2) // count
    depth = min(layers - 1, (wide - 1 + reach) // wide)
    pieces = PIECES
    fold = columns == 2 and depth == layers - 1 and depth >= 2 and layers * wide == pairs and pairs * count == BAND
    spectra = whiten(records, live_mask).reshape(count, windows * 8, LANES)
    slots = (depth + 1) * wide
    cross = pl.pallas_call(
        functools.partial(reach_kernel, (layers, columns, depth, pieces, windows, fold)),
        out_shape=jax.ShapeDtypeStruct((count, pairs, 8, LANES), jnp.float32),
        in_specs=[
            pl.BlockSpec(memory_space=pltpu.SMEM),
            pl.BlockSpec(memory_space=pltpu.VMEM),
        ],
        out_specs=pl.BlockSpec(memory_space=pltpu.VMEM),
        scratch_shapes=[
            pltpu.VMEM((slots + wide, count, windows * 8, LANES), jnp.bfloat16),
            pltpu.VMEM((slots * count, windows * 8, LANES), jnp.bfloat16),
            pltpu.VMEM((count, windows * 8, LANES), jnp.float32),
            pltpu.VMEM((count, windows * 8, LANES), jnp.float32),
            pltpu.VMEM((wide, count, 8, LANES), jnp.bfloat16),
            pltpu.VMEM((wide, count, 8, LANES), jnp.bfloat16),
        ]
        + [pltpu.SemaphoreType.DMA((depth + 2, pieces))] * 8
        + [pltpu.SemaphoreType.DMA((wide,))] * 2,
        compiler_params=pltpu.CompilerParams(
            vmem_limit_bytes=40 * 1024 * 1024, collective_id=0, has_side_effects=True
        ),
    )(offsets, spectra)
    cross = cross.astype(jnp.bfloat16).reshape(count * pairs, 8 * LANES)
    result = jnp.dot(cross, jnp.asarray(inverse_table(length)), preferred_element_type=jnp.float32)
    result = result * (1.0 / math.sqrt(F))
    return result.reshape(count, pairs, LAGS).astype(jnp.bfloat16)


def solution(mesh):
    in_specs = (P(("day", "chan"), None, None), P(("day", "chan")), P())
    out_specs = P(("day", "chan"), None, None)
    columns = max(1, LAYER_CHIPS // mesh.shape["day"])
    body = functools.partial(shards, columns)
    return jax.shard_map(body, mesh=mesh, in_specs=in_specs, out_specs=out_specs, check_vma=False)
```

```python
import functools
import math

import jax
import jax.numpy as jnp
import numpy as np
from jax import lax
from jax.experimental import pallas as pl
from jax.experimental.pallas import tpu as pltpu
from jax.sharding import PartitionSpec as P

F = 512
F0 = 6
LAGS = 2048
LANES = 128
BAND = 512
PIECES = 2
LAYER_CHIPS = 4


def forward_table(length):
    samples = np.arange(length, dtype=np.int64)
    freqs = F0 + np.arange(F, dtype=np.int64)
    phase = np.mod(samples[:, None] * freqs[None, :], length)
    angle = 2.0 * math.pi / length * phase
    return np.concatenate([np.cos(angle), -np.sin(angle)], axis=1).astype(np.float32).astype(jnp.bfloat16)


def inverse_table(length):
    freqs = F0 + np.arange(F, dtype=np.int64)
    shifts = np.arange(LAGS, dtype=np.int64) - LAGS // 2
    phase = np.mod(freqs[:, None] * shifts[None, :], length)
    angle = 2.0 * math.pi / length * phase
    return np.concatenate([np.cos(angle), -np.sin(angle)], axis=0).astype(np.float32).astype(jnp.bfloat16)


def whiten(records, live_mask):
    count, windows, length = records.shape
    spectrum = jnp.dot(
        records.reshape(count * windows, length),
        jnp.asarray(forward_table(length)),
        preferred_element_type=jnp.float32,
    )
    power = jnp.mean(spectrum * spectrum, axis=1, keepdims=True)
    gain = jnp.repeat(live_mask.astype(jnp.float32), windows)[:, None]
    white = spectrum * (gain * lax.rsqrt(power + 1e-06))
    return white.astype(jnp.bfloat16)


def reach_kernel(shape, offsets_ref, white_ref, cross_ref, held, ext, own, swapped, made, back,
                 z_send, z_recv, c_send, c_recv, y_send, y_recv, d_send, d_recv, r_send, r_recv):
    layers, columns, depth, pieces, windows, fold = shape
    count, slab = white_ref.shape[0], white_ref.shape[1]
    pairs = offsets_ref.shape[0]
    wide = 2 * columns
    total = layers * wide * count
    me = lax.axis_index("chan")
    z, q = me // wide, me % wide
    y, c = q // 2, q % 2
    sibling = me + 1 - 2 * c
    sib_q = q + 1 - 2 * c
    mate = me + 2 - 4 * y
    mate_q = q + 2 - 4 * y
    far_q = sib_q + 2 - 4 * y
    step = count // pieces
    top, lifted = layers - 1, depth + 1

    barrier = pltpu.get_barrier_semaphore()

    def greet(device):
        pl.semaphore_signal(barrier, inc=1, device_id={"chan": device}, device_id_type=pl.DeviceIdType.MESH)

    greet(sibling)
    if columns == 2:
        greet(mate)

    @pl.when(z >= 1)
    def _():
        greet(me - wide)

    @pl.when(z < layers - 1)
    def _():
        greet(me + wide)

    below, above = jnp.minimum(z, 1), jnp.minimum(top - z, 1)
    peers = columns + below + above
    if fold:
        @pl.when(z == 0)
        def _():
            for i in range(wide):
                greet(top * wide + i)

        @pl.when(z == top)
        def _():
            for i in range(wide):
                greet(jnp.int32(i))

        peers = peers + wide * (2 - below - above)
    pl.semaphore_wait(barrier, peers)

    def rows(p):
        return pl.ds(p * step, step)

    def mine(dz, p):
        return white_ref.at[rows(p)] if dz == 0 else held.at[dz * wide + q, rows(p)]

    def copy(source, slot, p, send, recv, device):
        return pltpu.make_async_remote_copy(
            src_ref=source,
            dst_ref=held.at[slot, rows(p)],
            send_sem=send,
            recv_sem=recv,
            device_id={"chan": device},
            device_id_type=pl.DeviceIdType.MESH,
        )

    def down(dz, p):
        return copy(mine(dz, p), (dz + 1) * wide + q, p, z_send.at[dz, p], z_recv.at[dz + 1, p], me - wide)

    def from_above(dz, p):
        return copy(mine(dz, p), dz * wide + q, p, z_send.at[dz, p], z_recv.at[dz, p], me)

    def across(dz, p, slot):
        return copy(mine(dz, p), slot, p, c_send.at[dz, p], c_recv.at[dz, p], sibling)

    def over(dz, p, slot):
        return copy(mine(dz, p), slot, p, y_send.at[dz, p], y_recv.at[dz, p], mate)

    def onward(dz, p, slot):
        return copy(held.at[dz * wide + mate_q, rows(p)], slot, p, d_send.at[dz, p], d_recv.at[dz, p], sibling)

    def both(*conditions):
        joined = conditions[0]
        for condition in conditions[1:]:
            joined = jnp.logical_and(joined, condition)
        return joined

    def exists(dz):
        return z + dz < layers

    def goes(dz, at_start, at_end):
        if dz == lifted:
            return z == top
        if dz == 0:
            return at_start
        if fold and dz == depth:
            return both(exists(dz), at_end)
        return exists(dz)

    def z_tx(dz):
        if fold and dz + 1 == depth:
            return both(exists(dz), z >= 1, jnp.logical_or(z >= 2, q == 0))
        return both(exists(dz), z >= 1)

    def z_rx(dz):
        return goes(dz, None, q == 0)

    def c_tx(dz):
        return goes(dz, c == 1, q == 0)

    def c_rx(dz):
        return goes(dz, c == 0, q == 1)

    def y_tx(dz):
        return goes(dz, y == 1, q == 0)

    def y_rx(dz):
        return goes(dz, y == 0, q == 2)

    def d_rx(dz):
        return goes(dz, y == 0, q == 3)

    def lift(p):
        return copy(white_ref.at[rows(p)], lifted * wide + q, p, z_send.at[lifted, p], z_recv.at[lifted, p],
                    me + top * wide)

    def sends(dz):
        for p in range(pieces):
            if dz > 0:
                @pl.when(z_rx(dz))
                def _():
                    from_above(dz, p).wait_recv()
            if dz < depth:
                @pl.when(z_tx(dz))
                def _():
                    down(dz, p).start()
            if columns == 2:
                @pl.when(y_tx(dz))
                def _():
                    over(dz, p, dz * wide + q).start()
            @pl.when(c_tx(dz))
            def _():
                across(dz, p, dz * wide + q).start()

    def passes(dz):
        if columns == 2:
            for p in range(pieces):
                @pl.when(y_rx(dz))
                def _():
                    over(dz, p, dz * wide + mate_q).wait_recv()
                    onward(dz, p, dz * wide + mate_q).start()

    def arrives(dz):
        for p in range(pieces):
            @pl.when(c_rx(dz))
            def _():
                across(dz, p, dz * wide + sib_q).wait_recv()
            if columns == 2:
                @pl.when(d_rx(dz))
                def _():
                    onward(dz, p, dz * wide + far_q).wait_recv()

    def finishes(dz):
        for p in range(pieces):
            if dz < depth:
                @pl.when(z_tx(dz))
                def _():
                    down(dz, p).wait_send()
            if columns == 2:
                @pl.when(y_tx(dz))
                def _():
                    over(dz, p, dz * wide + q).wait_send()
                @pl.when(y_rx(dz))
                def _():
                    onward(dz, p, dz * wide + mate_q).wait_send()
            @pl.when(c_tx(dz))
            def _():
                across(dz, p, dz * wide + q).wait_send()

    def answer(i):
        return pltpu.make_async_remote_copy(
            src_ref=made.at[i],
            dst_ref=back.at[q],
            send_sem=r_send.at[i],
            recv_sem=r_recv.at[q],
            device_id={"chan": jnp.int32(i)},
            device_id_type=pl.DeviceIdType.MESH,
        )

    def answered(i):
        return pltpu.make_async_remote_copy(
            src_ref=made.at[i],
            dst_ref=back.at[i],
            send_sem=r_send.at[i],
            recv_sem=r_recv.at[i],
            device_id={"chan": me},
            device_id_type=pl.DeviceIdType.MESH,
        )

    low = lax.broadcasted_iota(jnp.int32, (8, LANES), 0) < 4

    def prepare(i, carry):
        raw = white_ref[i]
        value = raw.astype(jnp.float32)
        own[i] = value
        ext[q * count + i] = raw
        for w in range(windows):
            swapped[i, w * 8 : w * 8 + 8] = pltpu.roll(value[w * 8 : w * 8 + 8], 4, 0)
        return carry

    def settle(dz):
        def one(l):
            def fill(i, carry):
                ext[(dz * wide + l) * count + i] = held[dz * wide + l, i]
                return carry
            lax.fori_loop(0, count, fill, 0, unroll=4)

        if dz == 0:
            for l in range(1, wide):
                @pl.when(q < l)
                def _():
                    one(l)
        else:
            @pl.when(exists(dz))
            def _():
                for l in range(1 if fold and dz == depth else wide):
                    one(l)

    live = jnp.minimum(layers * wide - me, pairs)

    def outside():
        def nothing(k, carry):
            for r in range(count):
                cross_ref[r, k] = jnp.zeros((8, LANES), jnp.float32)
            return carry

        lax.fori_loop(live, pairs, nothing, 0)

        @pl.when(layers - z <= depth)
        def _():
            def blank(i, carry):
                ext[(layers - z) * wide * count + i] = jnp.zeros((slab, LANES), jnp.bfloat16)
                return carry

            lax.fori_loop(0, 2 * count, blank, 0, unroll=4)

    def reached(dz):
        if dz < 0:
            return 0
        if dz == depth:
            return live
        return jnp.minimum((dz + 1) * wide - q - 1, live)

    def multiply(dz):
        def pair(k, carry):
            shift = offsets_ref[k]

            def channel(i, inner):
                place = me * count + i + shift
                keep = jnp.where(place < total, 1.0 / windows, 0.0)
                near = jnp.minimum(q * count + i + shift, ext.shape[0] - 1)
                partner = ext[near].astype(jnp.float32)
                straight = own[i, :8] * partner[:8]
                twisted = swapped[i, :8] * partner[:8]
                for w in range(1, windows):
                    part = slice(w * 8, w * 8 + 8)
                    straight += own[i, part] * partner[part]
                    twisted += swapped[i, part] * partner[part]
                joined = jnp.where(
                    low,
                    straight + pltpu.roll(straight, 4, 0),
                    pltpu.roll(twisted, 4, 0) - twisted,
                )
                cross_ref[i, k] = joined * keep
                return inner

            return lax.fori_loop(0, count, channel, carry, unroll=4)

        begin, end = reached(dz - 1), reached(dz)
        if fold and dz == depth:
            @pl.when(z == 0)
            def _():
                lax.fori_loop(begin, begin + 1, pair, 0)

            @pl.when(z > 0)
            def _():
                lax.fori_loop(begin, end, pair, 0)
        else:
            lax.fori_loop(begin, end, pair, 0)

    def reply():
        for i in range(wide):
            shift = offsets_ref[top * wide + q - i]

            def channel(r, carry):
                place = i * count + r + shift
                keep = jnp.where(place < total, 1.0 / windows, 0.0)
                near = jnp.clip(place - top * wide * count, 0, ext.shape[0] - 1)
                partner = ext[near].astype(jnp.float32)
                value = held[lifted * wide + i, r].astype(jnp.float32)
                straight = value[:8] * partner[:8]
                twisted = pltpu.roll(value[:8], 4, 0) * partner[:8]
                for w in range(1, windows):
                    part = slice(w * 8, w * 8 + 8)
                    straight += value[part] * partner[part]
                    twisted += pltpu.roll(value[part], 4, 0) * partner[part]
                joined = jnp.where(
                    low,
                    straight + pltpu.roll(straight, 4, 0),
                    pltpu.roll(twisted, 4, 0) - twisted,
                )
                made[i, r] = (joined * keep).astype(jnp.bfloat16)
                return carry

            lax.fori_loop(0, count, channel, 0, unroll=4)
        for i in range(wide):
            answer(i).start()

    sends(0)
    if fold:
        @pl.when(z == 0)
        def _():
            for p in range(pieces):
                lift(p).start()

    lax.fori_loop(0, count, prepare, 0)
    outside()
    for dz in range(depth + 1):
        if dz < depth:
            sends(dz + 1)
        if fold and dz == 0:
            sends(lifted)
        passes(dz)
        if fold and dz == 0:
            passes(lifted)
        arrives(dz)
        settle(dz)
        if fold and dz == 0:
            arrives(lifted)

            @pl.when(z == top)
            def _():
                reply()

        multiply(dz)

    if fold:
        @pl.when(z == 0)
        def _():
            for i in range(wide):
                answered(i).wait_recv()

                def take(r, carry):
                    cross_ref[r, top * wide - q + i] = back[i, r].astype(jnp.float32)
                    return carry

                lax.fori_loop(0, count, take, 0, unroll=4)
            for p in range(pieces):
                lift(p).wait_send()

        @pl.when(z == top)
        def _():
            for i in range(wide):
                answer(i).wait_send()

        finishes(lifted)
    for dz in range(depth + 1):
        finishes(dz)


def shards(columns, records, live_mask, offsets):
    count, windows, length = records.shape
    pairs = offsets.shape[0]
    wide = 2 * columns
    layers = lax.axis_size("chan") // wide
    reach = (BAND + count - 2) // count
    depth = min(layers - 1, (wide - 1 + reach) // wide)
    pieces = PIECES
    fold = columns == 2 and depth == layers - 1 and depth >= 2 and layers * wide == pairs and pairs * count == BAND
    spectra = whiten(records, live_mask).reshape(count, windows * 8, LANES)
    slots = (depth + 1) * wide
    cross = pl.pallas_call(
        functools.partial(reach_kernel, (layers, columns, depth, pieces, windows, fold)),
        out_shape=jax.ShapeDtypeStruct((count, pairs, 8, LANES), jnp.float32),
        in_specs=[
            pl.BlockSpec(memory_space=pltpu.SMEM),
            pl.BlockSpec(memory_space=pltpu.VMEM),
        ],
        out_specs=pl.BlockSpec(memory_space=pltpu.VMEM),
        scratch_shapes=[
            pltpu.VMEM((slots + wide, count, windows * 8, LANES), jnp.bfloat16),
            pltpu.VMEM((slots * count, windows * 8, LANES), jnp.bfloat16),
            pltpu.VMEM((count, windows * 8, LANES), jnp.float32),
            pltpu.VMEM((count, windows * 8, LANES), jnp.float32),
            pltpu.VMEM((wide, count, 8, LANES), jnp.bfloat16),
            pltpu.VMEM((wide, count, 8, LANES), jnp.bfloat16),
        ]
        + [pltpu.SemaphoreType.DMA((depth + 2, pieces))] * 8
        + [pltpu.SemaphoreType.DMA((wide,))] * 2,
        compiler_params=pltpu.CompilerParams(
            vmem_limit_bytes=40 * 1024 * 1024, collective_id=0, has_side_effects=True
        ),
    )(offsets, spectra)
    cross = cross.astype(jnp.bfloat16).reshape(count * pairs, 8 * LANES)
    result = jnp.dot(cross, jnp.asarray(inverse_table(length)), preferred_element_type=jnp.float32)
    result = result * (1.0 / math.sqrt(F))
    return result.reshape(count, pairs, LAGS).astype(jnp.bfloat16)


def solution(mesh):
    in_specs = (P(("day", "chan"), None, None), P(("day", "chan")), P())
    out_specs = P(("day", "chan"), None, None)
    columns = max(1, LAYER_CHIPS // mesh.shape["day"])
    body = functools.partial(shards, columns)
    return jax.shard_map(body, mesh=mesh, in_specs=in_specs, out_specs=out_specs, check_vma=False)
```

```python
import functools
import math

import jax
import jax.numpy as jnp
import numpy as np
from jax import lax
from jax.experimental import pallas as pl
from jax.experimental.pallas import tpu as pltpu
from jax.sharding import PartitionSpec as P

F = 512
F0 = 6
LAGS = 2048
LANES = 128
BAND = 512
PIECES = 4
LAYER_CHIPS = 4


def forward_table(length):
    samples = np.arange(length, dtype=np.int64)
    freqs = F0 + np.arange(F, dtype=np.int64)
    phase = np.mod(samples[:, None] * freqs[None, :], length)
    angle = 2.0 * math.pi / length * phase
    return np.concatenate([np.cos(angle), -np.sin(angle)], axis=1).astype(np.float32).astype(jnp.bfloat16)


def inverse_table(length):
    freqs = F0 + np.arange(F, dtype=np.int64)
    shifts = np.arange(LAGS, dtype=np.int64) - LAGS // 2
    phase = np.mod(freqs[:, None] * shifts[None, :], length)
    angle = 2.0 * math.pi / length * phase
    return np.concatenate([np.cos(angle), -np.sin(angle)], axis=0).astype(np.float32).astype(jnp.bfloat16)


def whiten(records, live_mask):
    count, windows, length = records.shape
    spectrum = jnp.dot(
        records.reshape(count * windows, length),
        jnp.asarray(forward_table(length)),
        preferred_element_type=jnp.float32,
    )
    power = jnp.mean(spectrum * spectrum, axis=1, keepdims=True)
    gain = jnp.repeat(live_mask.astype(jnp.float32), windows)[:, None]
    white = spectrum * (gain * lax.rsqrt(power + 1e-06))
    return white.astype(jnp.bfloat16)


def reach_kernel(shape, offsets_ref, white_ref, cross_ref, held, ext, own, swapped, made, back,
                 z_send, z_recv, c_send, c_recv, y_send, y_recv, d_send, d_recv, e_send, r_send, r_recv):
    layers, columns, depth, pieces, windows, fold = shape
    count, slab = white_ref.shape[0], white_ref.shape[1]
    pairs = offsets_ref.shape[0]
    wide = 2 * columns
    total = layers * wide * count
    me = lax.axis_index("chan")
    z, q = me // wide, me % wide
    y, c = q // 2, q % 2
    sibling = me + 1 - 2 * c
    sib_q = q + 1 - 2 * c
    mate = me + 2 - 4 * y
    mate_q = q + 2 - 4 * y
    far_q = sib_q + 2 - 4 * y
    step = count // pieces
    top, lifted = layers - 1, depth + 1

    barrier = pltpu.get_barrier_semaphore()

    def greet(device):
        pl.semaphore_signal(barrier, inc=1, device_id={"chan": device}, device_id_type=pl.DeviceIdType.MESH)

    greet(sibling)
    if columns == 2:
        greet(mate)

    @pl.when(z >= 1)
    def _():
        greet(me - wide)

    @pl.when(z < layers - 1)
    def _():
        greet(me + wide)

    below, above = jnp.minimum(z, 1), jnp.minimum(top - z, 1)
    peers = columns + below + above
    if fold:
        @pl.when(z == 0)
        def _():
            for i in range(wide):
                greet(top * wide + i)

        @pl.when(z == top)
        def _():
            for i in range(wide):
                greet(jnp.int32(i))

        peers = peers + wide * (2 - below - above)
    pl.semaphore_wait(barrier, peers)

    def rows(p):
        return pl.ds(p * step, step)

    def mine(dz, p):
        return white_ref.at[rows(p)] if dz == 0 else held.at[dz * wide + q, rows(p)]

    def copy(source, slot, p, send, recv, device):
        return pltpu.make_async_remote_copy(
            src_ref=source,
            dst_ref=held.at[slot, rows(p)],
            send_sem=send,
            recv_sem=recv,
            device_id={"chan": device},
            device_id_type=pl.DeviceIdType.MESH,
        )

    def down(dz, p):
        return copy(mine(dz, p), (dz + 1) * wide + q, p, z_send.at[dz, p], z_recv.at[dz + 1, p], me - wide)

    def from_above(dz, p):
        return copy(mine(dz, p), dz * wide + q, p, z_send.at[dz, p], z_recv.at[dz, p], me)

    def across(dz, p, slot):
        return copy(mine(dz, p), slot, p, c_send.at[dz, p], c_recv.at[dz, p], sibling)

    def over(dz, p, slot):
        return copy(mine(dz, p), slot, p, y_send.at[dz, p], y_recv.at[dz, p], mate)

    def onward(dz, p, slot):
        return copy(held.at[dz * wide + mate_q, rows(p)], slot, p, d_send.at[dz, p], d_recv.at[dz, p], sibling)

    def both(*conditions):
        joined = conditions[0]
        for condition in conditions[1:]:
            joined = jnp.logical_and(joined, condition)
        return joined

    def exists(dz):
        return z + dz < layers

    def goes(dz, at_start, at_end):
        if dz == lifted:
            return z == top
        if dz == 0:
            return at_start
        if fold and dz == depth:
            return both(exists(dz), at_end)
        return exists(dz)

    def z_tx(dz):
        if fold and dz + 1 == depth:
            return both(exists(dz), z >= 1, jnp.logical_or(z >= 2, q == 0))
        return both(exists(dz), z >= 1)

    def z_rx(dz):
        return goes(dz, None, q == 0)

    def c_tx(dz):
        return goes(dz, c == 1, q == 0)

    def c_rx(dz):
        return goes(dz, c == 0, q == 1)

    def y_tx(dz):
        return goes(dz, y == 1, q == 0)

    def y_rx(dz):
        return goes(dz, y == 0, q == 2)

    def detoured(dz, p):
        return fold and dz == depth - 1 and p == pieces - 1

    def over_tx(dz, p):
        if detoured(dz, p):
            return both(y_tx(dz), jnp.logical_or(z > 0, y == 0))
        return y_tx(dz)

    def extra(dz, p):
        return copy(held.at[dz * wide + mate_q, rows(p)], (dz + 1) * wide + mate_q, p,
                    e_send.at[dz, p], y_recv.at[dz + 1, p], me - wide)

    def extra_tx():
        return both(z == 1, y == 0)

    def d_rx(dz):
        return goes(dz, y == 0, q == 3)

    def lift(p):
        return copy(white_ref.at[rows(p)], lifted * wide + q, p, z_send.at[lifted, p], z_recv.at[lifted, p],
                    me + top * wide)

    def sends(dz):
        for p in range(pieces):
            if dz > 0:
                @pl.when(z_rx(dz))
                def _():
                    from_above(dz, p).wait_recv()
            if dz < depth:
                @pl.when(z_tx(dz))
                def _():
                    down(dz, p).start()
            if columns == 2:
                @pl.when(over_tx(dz, p))
                def _():
                    over(dz, p, dz * wide + q).start()
            @pl.when(c_tx(dz))
            def _():
                across(dz, p, dz * wide + q).start()

    def passes(dz):
        if columns == 2:
            for p in range(pieces):
                @pl.when(y_rx(dz))
                def _():
                    over(dz, p, dz * wide + mate_q).wait_recv()
                    onward(dz, p, dz * wide + mate_q).start()
                if detoured(dz + 1, p):
                    @pl.when(extra_tx())
                    def _():
                        extra(dz, p).start()

    def arrives(dz):
        for p in range(pieces):
            @pl.when(c_rx(dz))
            def _():
                across(dz, p, dz * wide + sib_q).wait_recv()
            if columns == 2:
                @pl.when(d_rx(dz))
                def _():
                    onward(dz, p, dz * wide + far_q).wait_recv()

    def finishes(dz):
        for p in range(pieces):
            if dz < depth:
                @pl.when(z_tx(dz))
                def _():
                    down(dz, p).wait_send()
            if columns == 2:
                @pl.when(over_tx(dz, p))
                def _():
                    over(dz, p, dz * wide + q).wait_send()
                if detoured(dz + 1, p):
                    @pl.when(extra_tx())
                    def _():
                        extra(dz, p).wait_send()
                @pl.when(y_rx(dz))
                def _():
                    onward(dz, p, dz * wide + mate_q).wait_send()
            @pl.when(c_tx(dz))
            def _():
                across(dz, p, dz * wide + q).wait_send()

    def answer(i):
        return pltpu.make_async_remote_copy(
            src_ref=made.at[i],
            dst_ref=back.at[q],
            send_sem=r_send.at[i],
            recv_sem=r_recv.at[q],
            device_id={"chan": jnp.int32(i)},
            device_id_type=pl.DeviceIdType.MESH,
        )

    def answered(i):
        return pltpu.make_async_remote_copy(
            src_ref=made.at[i],
            dst_ref=back.at[i],
            send_sem=r_send.at[i],
            recv_sem=r_recv.at[i],
            device_id={"chan": me},
            device_id_type=pl.DeviceIdType.MESH,
        )

    low = lax.broadcasted_iota(jnp.int32, (8, LANES), 0) < 4

    def prepare(i, carry):
        raw = white_ref[i]
        value = raw.astype(jnp.float32)
        own[i] = value
        ext[q * count + i] = raw
        for w in range(windows):
            swapped[i, w * 8 : w * 8 + 8] = pltpu.roll(value[w * 8 : w * 8 + 8], 4, 0)
        return carry

    def settle(dz):
        def one(l):
            def fill(i, carry):
                ext[(dz * wide + l) * count + i] = held[dz * wide + l, i]
                return carry
            lax.fori_loop(0, count, fill, 0, unroll=4)

        if dz == 0:
            for l in range(1, wide):
                @pl.when(q < l)
                def _():
                    one(l)
        else:
            @pl.when(exists(dz))
            def _():
                for l in range(1 if fold and dz == depth else wide):
                    one(l)

    live = jnp.minimum(layers * wide - me, pairs)

    def outside():
        def nothing(k, carry):
            for r in range(count):
                cross_ref[r, k] = jnp.zeros((8, LANES), jnp.float32)
            return carry

        lax.fori_loop(live, pairs, nothing, 0)

        @pl.when(layers - z <= depth)
        def _():
            def blank(i, carry):
                ext[(layers - z) * wide * count + i] = jnp.zeros((slab, LANES), jnp.bfloat16)
                return carry

            lax.fori_loop(0, 2 * count, blank, 0, unroll=4)

    def reached(dz):
        if dz < 0:
            return 0
        if dz == depth:
            return live
        return jnp.minimum((dz + 1) * wide - q - 1, live)

    def multiply(dz):
        def pair(k, carry):
            shift = offsets_ref[k]

            def channel(i, inner):
                place = me * count + i + shift
                keep = jnp.where(place < total, 1.0 / windows, 0.0)
                near = jnp.minimum(q * count + i + shift, ext.shape[0] - 1)
                partner = ext[near].astype(jnp.float32)
                straight = own[i, :8] * partner[:8]
                twisted = swapped[i, :8] * partner[:8]
                for w in range(1, windows):
                    part = slice(w * 8, w * 8 + 8)
                    straight += own[i, part] * partner[part]
                    twisted += swapped[i, part] * partner[part]
                joined = jnp.where(
                    low,
                    straight + pltpu.roll(straight, 4, 0),
                    pltpu.roll(twisted, 4, 0) - twisted,
                )
                cross_ref[i, k] = joined * keep
                return inner

            return lax.fori_loop(0, count, channel, carry, unroll=4)

        begin, end = reached(dz - 1), reached(dz)
        if fold and dz == depth:
            @pl.when(z == 0)
            def _():
                lax.fori_loop(begin, begin + 1, pair, 0)

            @pl.when(z > 0)
            def _():
                lax.fori_loop(begin, end, pair, 0)
        else:
            lax.fori_loop(begin, end, pair, 0)

    def reply():
        for i in range(wide):
            shift = offsets_ref[top * wide + q - i]

            def channel(r, carry):
                place = i * count + r + shift
                keep = jnp.where(place < total, 1.0 / windows, 0.0)
                near = jnp.clip(place - top * wide * count, 0, ext.shape[0] - 1)
                partner = ext[near].astype(jnp.float32)
                value = held[lifted * wide + i, r].astype(jnp.float32)
                straight = value[:8] * partner[:8]
                twisted = pltpu.roll(value[:8], 4, 0) * partner[:8]
                for w in range(1, windows):
                    part = slice(w * 8, w * 8 + 8)
                    straight += value[part] * partner[part]
                    twisted += pltpu.roll(value[part], 4, 0) * partner[part]
                joined = jnp.where(
                    low,
                    straight + pltpu.roll(straight, 4, 0),
                    pltpu.roll(twisted, 4, 0) - twisted,
                )
                made[i, r] = (joined * keep).astype(jnp.bfloat16)
                return carry

            lax.fori_loop(0, count, channel, 0, unroll=4)
        for i in range(wide):
            answer(i).start()

    sends(0)
    if fold:
        @pl.when(z == 0)
        def _():
            for p in range(pieces):
                lift(p).start()

    lax.fori_loop(0, count, prepare, 0)
    outside()
    for dz in range(depth + 1):
        if dz < depth:
            sends(dz + 1)
        if fold and dz == 0:
            sends(lifted)
        passes(dz)
        if fold and dz == 0:
            passes(lifted)
        arrives(dz)
        settle(dz)
        if fold and dz == 0:
            arrives(lifted)

            @pl.when(z == top)
            def _():
                reply()

        multiply(dz)

    if fold:
        @pl.when(z == 0)
        def _():
            for i in range(wide):
                answered(i).wait_recv()

                def take(r, carry):
                    cross_ref[r, top * wide - q + i] = back[i, r].astype(jnp.float32)
                    return carry

                lax.fori_loop(0, count, take, 0, unroll=4)
            for p in range(pieces):
                lift(p).wait_send()

        @pl.when(z == top)
        def _():
            for i in range(wide):
                answer(i).wait_send()

        finishes(lifted)
    for dz in range(depth + 1):
        finishes(dz)


def shards(columns, records, live_mask, offsets):
    count, windows, length = records.shape
    pairs = offsets.shape[0]
    wide = 2 * columns
    layers = lax.axis_size("chan") // wide
    reach = (BAND + count - 2) // count
    depth = min(layers - 1, (wide - 1 + reach) // wide)
    pieces = PIECES
    fold = columns == 2 and depth == layers - 1 and depth >= 2 and layers * wide == pairs and pairs * count == BAND
    spectra = whiten(records, live_mask).reshape(count, windows * 8, LANES)
    slots = (depth + 1) * wide
    cross = pl.pallas_call(
        functools.partial(reach_kernel, (layers, columns, depth, pieces, windows, fold)),
        out_shape=jax.ShapeDtypeStruct((count, pairs, 8, LANES), jnp.float32),
        in_specs=[
            pl.BlockSpec(memory_space=pltpu.SMEM),
            pl.BlockSpec(memory_space=pltpu.VMEM),
        ],
        out_specs=pl.BlockSpec(memory_space=pltpu.VMEM),
        scratch_shapes=[
            pltpu.VMEM((slots + wide, count, windows * 8, LANES), jnp.bfloat16),
            pltpu.VMEM((slots * count, windows * 8, LANES), jnp.bfloat16),
            pltpu.VMEM((count, windows * 8, LANES), jnp.float32),
            pltpu.VMEM((count, windows * 8, LANES), jnp.float32),
            pltpu.VMEM((wide, count, 8, LANES), jnp.bfloat16),
            pltpu.VMEM((wide, count, 8, LANES), jnp.bfloat16),
        ]
        + [pltpu.SemaphoreType.DMA((depth + 2, pieces))] * 9
        + [pltpu.SemaphoreType.DMA((wide,))] * 2,
        compiler_params=pltpu.CompilerParams(
            vmem_limit_bytes=40 * 1024 * 1024, collective_id=0, has_side_effects=True
        ),
    )(offsets, spectra)
    cross = cross.astype(jnp.bfloat16).reshape(count * pairs, 8 * LANES)
    result = jnp.dot(cross, jnp.asarray(inverse_table(length)), preferred_element_type=jnp.float32)
    result = result * (1.0 / math.sqrt(F))
    return result.reshape(count, pairs, LAGS).astype(jnp.bfloat16)


def solution(mesh):
    in_specs = (P(("day", "chan"), None, None), P(("day", "chan")), P())
    out_specs = P(("day", "chan"), None, None)
    columns = max(1, LAYER_CHIPS // mesh.shape["day"])
    body = functools.partial(shards, columns)
    return jax.shard_map(body, mesh=mesh, in_specs=in_specs, out_specs=out_specs, check_vma=False)
```

```python
import functools
import math

import jax
import jax.numpy as jnp
import numpy as np
from jax import lax
from jax.experimental import pallas as pl
from jax.experimental.pallas import tpu as pltpu
from jax.sharding import PartitionSpec as P

F = 512
F0 = 6
LAGS = 2048
LANES = 128
BAND = 512
PIECES = 4
LAYER_CHIPS = 4


def forward_table(length):
    samples = np.arange(length, dtype=np.int64)
    freqs = F0 + np.arange(F, dtype=np.int64)
    phase = np.mod(samples[:, None] * freqs[None, :], length)
    angle = 2.0 * math.pi / length * phase
    return np.concatenate([np.cos(angle), -np.sin(angle)], axis=1).astype(np.float32).astype(jnp.bfloat16)


def inverse_table(length):
    freqs = F0 + np.arange(F, dtype=np.int64)
    shifts = np.arange(LAGS, dtype=np.int64) - LAGS // 2
    phase = np.mod(freqs[:, None] * shifts[None, :], length)
    angle = 2.0 * math.pi / length * phase
    return np.concatenate([np.cos(angle), -np.sin(angle)], axis=0).astype(np.float32).astype(jnp.bfloat16)


def whiten(records, live_mask):
    count, windows, length = records.shape
    spectrum = jnp.dot(
        records.reshape(count * windows, length),
        jnp.asarray(forward_table(length)),
        preferred_element_type=jnp.float32,
    )
    power = jnp.mean(spectrum * spectrum, axis=1, keepdims=True)
    gain = jnp.repeat(live_mask.astype(jnp.float32), windows)[:, None]
    white = spectrum * (gain * lax.rsqrt(power + 1e-06))
    return white.astype(jnp.bfloat16)


def reach_kernel(shape, offsets_ref, white_ref, cross_ref, held, ext, own, swapped, made, back,
                 z_send, z_recv, c_send, c_recv, y_send, y_recv, d_send, d_recv, e_send, r_send, r_recv):
    layers, columns, depth, pieces, windows, fold = shape
    count, slab = white_ref.shape[0], white_ref.shape[1]
    pairs = offsets_ref.shape[0]
    wide = 2 * columns
    total = layers * wide * count
    me = lax.axis_index("chan")
    z, q = me // wide, me % wide
    y, c = q // 2, q % 2
    sibling = me + 1 - 2 * c
    sib_q = q + 1 - 2 * c
    mate = me + 2 - 4 * y
    mate_q = q + 2 - 4 * y
    far_q = sib_q + 2 - 4 * y
    step = count // pieces
    top, lifted = layers - 1, depth + 1

    barrier = pltpu.get_barrier_semaphore()

    def greet(device):
        pl.semaphore_signal(barrier, inc=1, device_id={"chan": device}, device_id_type=pl.DeviceIdType.MESH)

    greet(sibling)
    if columns == 2:
        greet(mate)

    @pl.when(z >= 1)
    def _():
        greet(me - wide)

    @pl.when(z < layers - 1)
    def _():
        greet(me + wide)

    below, above = jnp.minimum(z, 1), jnp.minimum(top - z, 1)
    peers = columns + below + above
    if fold:
        @pl.when(z == 0)
        def _():
            for i in range(wide):
                greet(top * wide + i)

        @pl.when(z == top)
        def _():
            for i in range(wide):
                greet(jnp.int32(i))

        peers = peers + wide * (2 - below - above)
    pl.semaphore_wait(barrier, peers)

    def rows(p):
        return pl.ds(p * step, step)

    def mine(dz, p):
        return white_ref.at[rows(p)] if dz == 0 else held.at[dz * wide + q, rows(p)]

    def copy(source, slot, p, send, recv, device):
        return pltpu.make_async_remote_copy(
            src_ref=source,
            dst_ref=held.at[slot, rows(p)],
            send_sem=send,
            recv_sem=recv,
            device_id={"chan": device},
            device_id_type=pl.DeviceIdType.MESH,
        )

    def down(dz, p):
        return copy(mine(dz, p), (dz + 1) * wide + q, p, z_send.at[dz, p], z_recv.at[dz + 1, p], me - wide)

    def from_above(dz, p):
        return copy(mine(dz, p), dz * wide + q, p, z_send.at[dz, p], z_recv.at[dz, p], me)

    def across(dz, p, slot):
        return copy(mine(dz, p), slot, p, c_send.at[dz, p], c_recv.at[dz, p], sibling)

    def over(dz, p, slot):
        return copy(mine(dz, p), slot, p, y_send.at[dz, p], y_recv.at[dz, p], mate)

    def onward(dz, p, slot):
        return copy(held.at[dz * wide + mate_q, rows(p)], slot, p, d_send.at[dz, p], d_recv.at[dz, p], sibling)

    def both(*conditions):
        joined = conditions[0]
        for condition in conditions[1:]:
            joined = jnp.logical_and(joined, condition)
        return joined

    def exists(dz):
        return z + dz < layers

    def goes(dz, at_start, at_end):
        if dz == lifted:
            return z == top
        if dz == 0:
            return at_start
        if fold and dz == depth:
            return both(exists(dz), at_end)
        return exists(dz)

    def z_tx(dz):
        if fold and dz + 1 == depth:
            return both(exists(dz), z >= 1, jnp.logical_or(z >= 2, q == 0))
        return both(exists(dz), z >= 1)

    def z_rx(dz):
        return goes(dz, None, q == 0)

    def c_tx(dz):
        return goes(dz, c == 1, q == 0)

    def c_rx(dz):
        return goes(dz, c == 0, q == 1)

    def y_tx(dz):
        return goes(dz, y == 1, q == 0)

    def y_rx(dz):
        return goes(dz, y == 0, q == 2)

    def detoured(dz, p):
        return fold and dz == depth - 1 and p == pieces - 1

    def over_tx(dz, p):
        if detoured(dz, p):
            return both(y_tx(dz), jnp.logical_or(z > 0, y == 0))
        if raised(dz, p):
            return both(y_tx(dz), y == 0)
        return y_tx(dz)

    def raised(dz, p):
        return fold and dz == lifted and p >= pieces // 2

    def lift_mate(p):
        return copy(held.at[mate_q, rows(p)], lifted * wide + mate_q, p,
                    e_send.at[lifted, p], y_recv.at[lifted, p], me + top * wide)

    def extra(dz, p):
        return copy(held.at[dz * wide + mate_q, rows(p)], (dz + 1) * wide + mate_q, p,
                    e_send.at[dz, p], y_recv.at[dz + 1, p], me - wide)

    def extra_tx():
        return both(z == 1, y == 0)

    def d_rx(dz):
        return goes(dz, y == 0, q == 3)

    def lift(p):
        return copy(white_ref.at[rows(p)], lifted * wide + q, p, z_send.at[lifted, p], z_recv.at[lifted, p],
                    me + top * wide)

    def sends(dz):
        for p in range(pieces):
            if dz > 0:
                @pl.when(z_rx(dz))
                def _():
                    from_above(dz, p).wait_recv()
            if dz < depth:
                @pl.when(z_tx(dz))
                def _():
                    down(dz, p).start()
            if columns == 2:
                @pl.when(over_tx(dz, p))
                def _():
                    over(dz, p, dz * wide + q).start()
            @pl.when(c_tx(dz))
            def _():
                across(dz, p, dz * wide + q).start()

    def passes(dz):
        if columns == 2:
            for p in range(pieces):
                @pl.when(y_rx(dz))
                def _():
                    over(dz, p, dz * wide + mate_q).wait_recv()
                    onward(dz, p, dz * wide + mate_q).start()
                if dz == 0 and raised(lifted, p):
                    @pl.when(both(z == 0, y == 0))
                    def _():
                        lift_mate(p).start()
                if detoured(dz + 1, p):
                    @pl.when(extra_tx())
                    def _():
                        extra(dz, p).start()

    def arrives(dz):
        for p in range(pieces):
            @pl.when(c_rx(dz))
            def _():
                across(dz, p, dz * wide + sib_q).wait_recv()
            if columns == 2:
                @pl.when(d_rx(dz))
                def _():
                    onward(dz, p, dz * wide + far_q).wait_recv()

    def finishes(dz):
        for p in range(pieces):
            if dz < depth:
                @pl.when(z_tx(dz))
                def _():
                    down(dz, p).wait_send()
            if columns == 2:
                @pl.when(over_tx(dz, p))
                def _():
                    over(dz, p, dz * wide + q).wait_send()
                if detoured(dz + 1, p):
                    @pl.when(extra_tx())
                    def _():
                        extra(dz, p).wait_send()
                @pl.when(y_rx(dz))
                def _():
                    onward(dz, p, dz * wide + mate_q).wait_send()
            @pl.when(c_tx(dz))
            def _():
                across(dz, p, dz * wide + q).wait_send()

    def answer(i):
        return pltpu.make_async_remote_copy(
            src_ref=made.at[i],
            dst_ref=back.at[q],
            send_sem=r_send.at[i],
            recv_sem=r_recv.at[q],
            device_id={"chan": jnp.int32(i)},
            device_id_type=pl.DeviceIdType.MESH,
        )

    def answered(i):
        return pltpu.make_async_remote_copy(
            src_ref=made.at[i],
            dst_ref=back.at[i],
            send_sem=r_send.at[i],
            recv_sem=r_recv.at[i],
            device_id={"chan": me},
            device_id_type=pl.DeviceIdType.MESH,
        )

    low = lax.broadcasted_iota(jnp.int32, (8, LANES), 0) < 4

    def prepare(i, carry):
        raw = white_ref[i]
        value = raw.astype(jnp.float32)
        own[i] = value
        ext[q * count + i] = raw
        for w in range(windows):
            swapped[i, w * 8 : w * 8 + 8] = pltpu.roll(value[w * 8 : w * 8 + 8], 4, 0)
        return carry

    def settle(dz):
        def one(l):
            def fill(i, carry):
                ext[(dz * wide + l) * count + i] = held[dz * wide + l, i]
                return carry
            lax.fori_loop(0, count, fill, 0, unroll=4)

        if dz == 0:
            for l in range(1, wide):
                @pl.when(q < l)
                def _():
                    one(l)
        else:
            @pl.when(exists(dz))
            def _():
                for l in range(1 if fold and dz == depth else wide):
                    one(l)

    live = jnp.minimum(layers * wide - me, pairs)

    def outside():
        def nothing(k, carry):
            for r in range(count):
                cross_ref[r, k] = jnp.zeros((8, LANES), jnp.float32)
            return carry

        lax.fori_loop(live, pairs, nothing, 0)

        @pl.when(layers - z <= depth)
        def _():
            def blank(i, carry):
                ext[(layers - z) * wide * count + i] = jnp.zeros((slab, LANES), jnp.bfloat16)
                return carry

            lax.fori_loop(0, 2 * count, blank, 0, unroll=4)

    def reached(dz):
        if dz < 0:
            return 0
        if dz == depth:
            return live
        return jnp.minimum((dz + 1) * wide - q - 1, live)

    def multiply(dz):
        def pair(k, carry):
            shift = offsets_ref[k]

            def channel(i, inner):
                place = me * count + i + shift
                keep = jnp.where(place < total, 1.0 / windows, 0.0)
                near = jnp.minimum(q * count + i + shift, ext.shape[0] - 1)
                partner = ext[near].astype(jnp.float32)
                straight = own[i, :8] * partner[:8]
                twisted = swapped[i, :8] * partner[:8]
                for w in range(1, windows):
                    part = slice(w * 8, w * 8 + 8)
                    straight += own[i, part] * partner[part]
                    twisted += swapped[i, part] * partner[part]
                joined = jnp.where(
                    low,
                    straight + pltpu.roll(straight, 4, 0),
                    pltpu.roll(twisted, 4, 0) - twisted,
                )
                cross_ref[i, k] = joined * keep
                return inner

            return lax.fori_loop(0, count, channel, carry, unroll=4)

        begin, end = reached(dz - 1), reached(dz)
        if fold and dz == depth:
            @pl.when(z == 0)
            def _():
                lax.fori_loop(begin, begin + 1, pair, 0)

            @pl.when(z > 0)
            def _():
                lax.fori_loop(begin, end, pair, 0)
        else:
            lax.fori_loop(begin, end, pair, 0)

    def reply():
        for i in range(wide):
            shift = offsets_ref[top * wide + q - i]

            def channel(r, carry):
                place = i * count + r + shift
                keep = jnp.where(place < total, 1.0 / windows, 0.0)
                near = jnp.clip(place - top * wide * count, 0, ext.shape[0] - 1)
                partner = ext[near].astype(jnp.float32)
                value = held[lifted * wide + i, r].astype(jnp.float32)
                straight = value[:8] * partner[:8]
                twisted = pltpu.roll(value[:8], 4, 0) * partner[:8]
                for w in range(1, windows):
                    part = slice(w * 8, w * 8 + 8)
                    straight += value[part] * partner[part]
                    twisted += pltpu.roll(value[part], 4, 0) * partner[part]
                joined = jnp.where(
                    low,
                    straight + pltpu.roll(straight, 4, 0),
                    pltpu.roll(twisted, 4, 0) - twisted,
                )
                made[i, r] = (joined * keep).astype(jnp.bfloat16)
                return carry

            lax.fori_loop(0, count, channel, 0, unroll=4)
        for i in range(wide):
            answer(i).start()

    sends(0)
    if fold:
        @pl.when(z == 0)
        def _():
            for p in range(pieces):
                lift(p).start()

    lax.fori_loop(0, count, prepare, 0)
    outside()
    for dz in range(depth + 1):
        if dz < depth:
            sends(dz + 1)
        if fold and dz == 0:
            sends(lifted)
        passes(dz)
        if fold and dz == 0:
            passes(lifted)
        arrives(dz)
        settle(dz)
        if fold and dz == 0:
            arrives(lifted)

            @pl.when(z == top)
            def _():
                reply()

        multiply(dz)

    if fold:
        @pl.when(z == 0)
        def _():
            for i in range(wide):
                answered(i).wait_recv()

                def take(r, carry):
                    cross_ref[r, top * wide - q + i] = back[i, r].astype(jnp.float32)
                    return carry

                lax.fori_loop(0, count, take, 0, unroll=4)
            for p in range(pieces):
                lift(p).wait_send()
                if raised(lifted, p):
                    @pl.when(y == 0)
                    def _():
                        lift_mate(p).wait_send()

        @pl.when(z == top)
        def _():
            for i in range(wide):
                answer(i).wait_send()

        finishes(lifted)
    for dz in range(depth + 1):
        finishes(dz)


def shards(columns, records, live_mask, offsets):
    count, windows, length = records.shape
    pairs = offsets.shape[0]
    wide = 2 * columns
    layers = lax.axis_size("chan") // wide
    reach = (BAND + count - 2) // count
    depth = min(layers - 1, (wide - 1 + reach) // wide)
    pieces = PIECES
    fold = columns == 2 and depth == layers - 1 and depth >= 2 and layers * wide == pairs and pairs * count == BAND
    spectra = whiten(records, live_mask).reshape(count, windows * 8, LANES)
    slots = (depth + 1) * wide
    cross = pl.pallas_call(
        functools.partial(reach_kernel, (layers, columns, depth, pieces, windows, fold)),
        out_shape=jax.ShapeDtypeStruct((count, pairs, 8, LANES), jnp.float32),
        in_specs=[
            pl.BlockSpec(memory_space=pltpu.SMEM),
            pl.BlockSpec(memory_space=pltpu.VMEM),
        ],
        out_specs=pl.BlockSpec(memory_space=pltpu.VMEM),
        scratch_shapes=[
            pltpu.VMEM((slots + wide, count, windows * 8, LANES), jnp.bfloat16),
            pltpu.VMEM((slots * count, windows * 8, LANES), jnp.bfloat16),
            pltpu.VMEM((count, windows * 8, LANES), jnp.float32),
            pltpu.VMEM((count, windows * 8, LANES), jnp.float32),
            pltpu.VMEM((wide, count, 8, LANES), jnp.bfloat16),
            pltpu.VMEM((wide, count, 8, LANES), jnp.bfloat16),
        ]
        + [pltpu.SemaphoreType.DMA((depth + 2, pieces))] * 9
        + [pltpu.SemaphoreType.DMA((wide,))] * 2,
        compiler_params=pltpu.CompilerParams(
            vmem_limit_bytes=40 * 1024 * 1024, collective_id=0, has_side_effects=True
        ),
    )(offsets, spectra)
    cross = cross.astype(jnp.bfloat16).reshape(count * pairs, 8 * LANES)
    result = jnp.dot(cross, jnp.asarray(inverse_table(length)), preferred_element_type=jnp.float32)
    result = result * (1.0 / math.sqrt(F))
    return result.reshape(count, pairs, LAGS).astype(jnp.bfloat16)


def solution(mesh):
    in_specs = (P(("day", "chan"), None, None), P(("day", "chan")), P())
    out_specs = P(("day", "chan"), None, None)
    columns = max(1, LAYER_CHIPS // mesh.shape["day"])
    body = functools.partial(shards, columns)
    return jax.shard_map(body, mesh=mesh, in_specs=in_specs, out_specs=out_specs, check_vma=False)
```
